32 devices in a mesh: wide: 8 (over z, x), narrow: 4 (over y, core).
Axes of the slice: x: 2, y: 2, z: 4, core: 2. Of those that a mesh axis runs over, the one named last changes fastest.
Arguments:
- displacement: float32 [3, 3, 128, 128, 384], P(None, None, 'wide', 'narrow'), may hold values from -6 to 6
- material: int32 [128, 128, 24], P('wide', 'narrow'), may hold values 0 or 1
- level_set: float32 [384, 128, 128], P('wide', 'narrow'), may hold values from -6 to 6
Outputs:
- level_next: float32 [384, 128, 128], P('wide', 'narrow')
- speed: float32 [384, 128, 128], P('wide', 'narrow')
The draws below stay inside these ranges and needn't reach their ends.
All inputs are finite; a program needn't handle non-finite values. No bound on the sum of `material` on one device may be relied on, other than what follows from the above.
Results may differ from the reference program's by a relative error of at most 0.00002.
Values sent between devices are 32-bit elements; how exact they have to be, the bound alone decides.
A program may use at most 192 MiB of HBM per device.

```python
import jax
import jax.numpy as jnp
from jax import lax

BZ = 16
EXT_PASSES = 4
HJ_STEPS = 3
NX = 128
NY = 128
NZ = 384


def set_ends(array, stream_key, smallest, high):
    extent = array.shape
    place = [jax.random.randint(jax.random.fold_in(stream_key, axis), (), 0, extent[axis]) for axis in range(len(extent))]
    array = array.at[tuple(place)].set(smallest)
    longest = extent.index(max(extent))
    place[longest] = (place[longest] + 1) % extent[longest]
    return array.at[tuple(place)].set(high)


def block_scale(rng, dims, cuts, least, high):
    loudness = 1.0
    for axis_at, blocks in cuts:
        heights = jax.random.uniform(jax.random.fold_in(jax.random.fold_in(rng, 6), axis_at), (blocks,), jnp.float32, least / len(cuts), high / len(cuts))
        loudness = loudness * jnp.repeat(jnp.exp(heights), dims[axis_at] // blocks).reshape((-1,) + (1,) * (len(dims) - 1 - axis_at))
    return loudness


def gaussian(stream_key, shape, scale, bound, cuts=(), held_as=jnp.bfloat16):
    array = jax.random.normal(stream_key, shape, jnp.float32) * scale
    if len(cuts) > 0:
        array = block_scale(stream_key, shape, cuts, -0.22, 0.18) * array
    return jnp.clip(array, min=-bound, max=bound).astype(held_as)


def setup_inputs(seed: int = 0) -> dict:
    streams_of = jax.random.split(jax.random.key(seed), 4)
    return {
        "displacement": gaussian(streams_of[0], (3, 3, NX, NY, NZ), 1.0, 6.0, ((2, 8), (3, 4)), jnp.float32),
        "material": set_ends((jax.random.randint(streams_of[1], (NX, NY, NZ // BZ), 0, 4) < 3).astype(jnp.int32), jax.random.fold_in(streams_of[1], 1), 0, 1),
        "level_set": gaussian(streams_of[2], (NZ, NY, NX), 1.0, 6.0, ((0, 8), (1, 4)), jnp.float32),
    }


SHEAR = 0.384615
LAME = 0.576923
WENO_EPS = 1e-06
TIME_STEP = 0.3
VAL_TAPS = (1.0 / 48.0, 23.0 / 48.0, 23.0 / 48.0, 1.0 / 48.0)
DER_TAPS = (-1.0 / 8.0, -5.0 / 8.0, 5.0 / 8.0, 1.0 / 8.0)

def apply_taps(padded, taps, axis, count):
    total = taps[0] * lax.slice_in_dim(padded, 1, 1 + count, axis=axis)
    for k in range(1, 4):
        total = total + taps[k] * lax.slice_in_dim(padded, 1 + k, 1 + k + count, axis=axis)
    return total

def strain_energy(grad_x, grad_y, grad_z, stiffness):
    exx = grad_x[:, 0]
    eyy = grad_y[:, 1]
    ezz = grad_z[:, 2]
    exy = 0.5 * (grad_y[:, 0] + grad_x[:, 1])
    exz = 0.5 * (grad_z[:, 0] + grad_x[:, 2])
    eyz = 0.5 * (grad_z[:, 1] + grad_y[:, 2])
    trace = exx + eyy + ezz
    square = exx * exx + eyy * eyy + ezz * ezz + 2.0 * (exy * exy + exz * exz + eyz * eyz)
    density = SHEAR * square + 0.5 * LAME * trace * trace
    return stiffness * lax.optimization_barrier(jnp.sum(density, axis=0))

def neighbour_mean(padded):
    wider = jnp.pad(padded, ((0, 0), (0, 0), (1, 1)))
    total = wider[2:, 1:-1, 1:-1] + wider[:-2, 1:-1, 1:-1]
    total = total + wider[1:-1, 2:, 1:-1] + wider[1:-1, :-2, 1:-1]
    total = total + wider[1:-1, 1:-1, 2:] + wider[1:-1, 1:-1, :-2]
    return total * (1.0 / 6.0)

def weno_side(v1, v2, v3, v4, v5):
    p_one = v1 / 3.0 - 7.0 * v2 / 6.0 + 11.0 * v3 / 6.0
    p_two = -v2 / 6.0 + 5.0 * v3 / 6.0 + v4 / 3.0
    p_three = v3 / 3.0 + 5.0 * v4 / 6.0 - v5 / 6.0
    b_one = 13.0 / 12.0 * (v1 - 2.0 * v2 + v3) ** 2 + 0.25 * (v1 - 4.0 * v2 + 3.0 * v3) ** 2
    b_two = 13.0 / 12.0 * (v2 - 2.0 * v3 + v4) ** 2 + 0.25 * (v2 - v4) ** 2
    b_three = 13.0 / 12.0 * (v3 - 2.0 * v4 + v5) ** 2 + 0.25 * (3.0 * v3 - 4.0 * v4 + v5) ** 2
    a_one = 0.1 / (WENO_EPS + b_one) ** 2
    a_two = 0.6 / (WENO_EPS + b_two) ** 2
    a_three = 0.3 / (WENO_EPS + b_three) ** 2
    return (a_one * p_one + a_two * p_two + a_three * p_three) / (a_one + a_two + a_three)

def march_step(padded, speed):
    wider = jnp.pad(padded, ((0, 0), (0, 0), (3, 3)), constant_values=1.0)
    size_z = padded.shape[0] - 6
    size_y = padded.shape[1] - 6
    size_x = padded.shape[2]
    centre = wider[3:3 + size_z, 3:3 + size_y, 3:3 + size_x]
    lines = (wider[:, 3:3 + size_y, 3:3 + size_x], wider[3:3 + size_z, :, 3:3 + size_x], wider[3:3 + size_z, 3:3 + size_y, :])
    grow_plus = None
    grow_minus = None
    for axis in range(3):
        line = lines[axis]
        count = centre.shape[axis]
        diffs = lax.slice_in_dim(line, 1, count + 6, axis=axis) - lax.slice_in_dim(line, 0, count + 5, axis=axis)
        parts = [lax.slice_in_dim(diffs, k, k + count, axis=axis) for k in range(6)]
        minus = weno_side(parts[0], parts[1], parts[2], parts[3], parts[4])
        plus = weno_side(parts[5], parts[4], parts[3], parts[2], parts[1])
        term_p = jnp.maximum(jnp.maximum(minus, 0.0) ** 2, jnp.minimum(plus, 0.0) ** 2)
        term_m = jnp.maximum(jnp.minimum(minus, 0.0) ** 2, jnp.maximum(plus, 0.0) ** 2)
        grow_plus = term_p if grow_plus is None else grow_plus + term_p
        grow_minus = term_m if grow_minus is None else grow_minus + term_m
    return centre - TIME_STEP * (jnp.maximum(speed, 0.0) * jnp.sqrt(grow_plus) + jnp.minimum(speed, 0.0) * jnp.sqrt(grow_minus))

def reference(displacement, material, level_set):
    padded = jnp.pad(displacement, ((0, 0), (0, 0), (2, 2), (2, 2), (2, 2)))
    size_x = displacement.shape[2]
    size_y = displacement.shape[3]
    size_z = displacement.shape[4]
    val_z = apply_taps(padded, VAL_TAPS, 4, size_z)
    der_z = apply_taps(padded, DER_TAPS, 4, size_z)
    vv = apply_taps(val_z, VAL_TAPS, 3, size_y)
    vd = apply_taps(val_z, DER_TAPS, 3, size_y)
    dv = apply_taps(der_z, VAL_TAPS, 3, size_y)
    grad_x = apply_taps(vv, DER_TAPS, 2, size_x)
    grad_y = apply_taps(vd, VAL_TAPS, 2, size_x)
    grad_z = apply_taps(dv, VAL_TAPS, 2, size_x)
    stiffness = 0.2 + 0.8 * jnp.repeat(material.astype(jnp.float32), BZ, axis=2)
    energy = strain_energy(grad_x, grad_y, grad_z, stiffness)
    peak = jnp.max(energy)
    velocity = jnp.transpose(energy / (peak + 1e-06) - 0.5, (2, 1, 0))
    weight = 1.0 / (1.0 + 4.0 * level_set * level_set)
    speed = velocity
    for step in range(EXT_PASSES):
        speed = weight * velocity + (1.0 - weight) * neighbour_mean(jnp.pad(speed, ((1, 1), (1, 1), (0, 0))))
    phi = level_set
    for step in range(HJ_STEPS):
        phi = march_step(jnp.pad(phi, ((3, 3), (3, 3), (0, 0)), constant_values=1.0), speed)
    return (phi, speed)
```

```python
import functools

import jax
import jax.numpy as jnp
from jax import lax
from jax.experimental import pallas as pl
from jax.experimental.pallas import tpu as pltpu
from jax.sharding import PartitionSpec as P

BZ = 16
EXT_PASSES = 4
HJ_STEPS = 3


SHEAR = 0.384615
LAME = 0.576923
WENO_EPS = 1e-06
TIME_STEP = 0.3
VAL_TAPS = (1.0 / 48.0, 23.0 / 48.0, 23.0 / 48.0, 1.0 / 48.0)
DER_TAPS = (-1.0 / 8.0, -5.0 / 8.0, 5.0 / 8.0, 1.0 / 8.0)


def with_halo(block, sides, width):
    for axis, dim in sides:
        count = lax.axis_size(axis)
        forward = [(i, i + 1) for i in range(count - 1)]
        backward = [(target, source) for source, target in forward]
        low = lax.ppermute(
            lax.slice_in_dim(block, block.shape[dim] - width, None, axis=dim), axis, forward
        )
        high = lax.ppermute(lax.slice_in_dim(block, 0, width, axis=dim), axis, backward)
        block = jnp.concatenate([low, block, high], axis=dim)
    return block


def shift_from(block, axis, dim, width, up):
    count = lax.axis_size(axis)
    if up:
        pairs = [(i, i + 1) for i in range(count - 1)]
        part = lax.slice_in_dim(block, block.shape[dim] - width, None, axis=dim)
    else:
        pairs = [(i + 1, i) for i in range(count - 1)]
        part = lax.slice_in_dim(block, 0, width, axis=dim)
    return lax.ppermute(part, axis, pairs)


def z_filters(u):
    size = u.shape[-1]
    lane = lax.broadcasted_iota(jnp.int32, u.shape, u.ndim - 1)
    last = u.ndim - 1
    before = jnp.where(lane == 0, 0.0, pltpu.roll(u, 1, last))
    after = jnp.where(lane == size - 1, 0.0, pltpu.roll(u, size - 1, last))
    second = jnp.where(lane >= size - 2, 0.0, pltpu.roll(u, size - 2, last))
    val = VAL_TAPS[0] * (before + second) + VAL_TAPS[1] * (u + after)
    der = DER_TAPS[3] * (second - before) + DER_TAPS[2] * (after - u)
    return val, der


def energy_kernel(own_ref, xh_ref, yh_ref, stiff_ref, out_ref, peak_ref, val_ref, der_ref):
    load = pl.program_id(0)
    size_x, size_y, size_z = own_ref.shape[2:]
    rows = val_ref.shape[2]

    def plane(c, p, body, tail):
        val, der = z_filters(body)
        val_ref[c, p, 0:size_y, :] = val
        der_ref[c, p, 0:size_y, :] = der
        val, der = z_filters(tail)
        val_ref[c, p, size_y:rows, :] = val
        der_ref[c, p, size_y:rows, :] = der

    for c in range(3):
        @pl.loop(0, size_x)
        def _(p):
            plane(c, p, own_ref[0, c, p], yh_ref[0, c, p])

        @pl.loop(0, 3)
        def _(q):
            plane(c, size_x + q, xh_ref[0, c, q], yh_ref[0, c, size_x + q])

    def taps_x(ref, c, idx, cols):
        parts = [ref[c, i, :, cols] for i in idx]
        return parts[0] + parts[3], parts[1] + parts[2], parts[3] - parts[0], parts[2] - parts[1]

    def along_y(val_part, der_part):
        total = None
        for k, shift in enumerate((1, 0, rows - 1, rows - 2)):
            term = None
            if val_part is not None:
                term = VAL_TAPS[k] * val_part
            if der_part is not None:
                extra = DER_TAPS[k] * der_part
                term = extra if term is None else term + extra
            if shift:
                term = pltpu.roll(term, shift, 0)
            total = term if total is None else total + term
        return total[0:size_y]

    chunk = 128

    @pl.loop(0, size_x)
    def _(p):
        low = jnp.where(p == 0, size_x + 2, p - 1)
        idx = (low, p, p + 1, p + 2)
        for piece in range(size_z // chunk):
            cols = pl.ds(piece * chunk, chunk)
            fields = []
            for c in range(3):
                outer, inner, far, near = taps_x(val_ref, c, idx, cols)
                vv = VAL_TAPS[0] * outer + VAL_TAPS[1] * inner
                dv = DER_TAPS[3] * far + DER_TAPS[2] * near
                outer, inner, _, _ = taps_x(der_ref, c, idx, cols)
                vz = VAL_TAPS[0] * outer + VAL_TAPS[1] * inner
                fields.append((vv, dv, vz))
            exx = along_y(fields[0][1], None)
            eyy = along_y(None, fields[1][0])
            ezz = along_y(fields[2][2], None)
            exy = 0.5 * along_y(fields[1][1], fields[0][0])
            exz = 0.5 * along_y(fields[0][2] + fields[2][1], None)
            eyz = 0.5 * along_y(fields[1][2], fields[2][0])
            trace = exx + eyy + ezz
            square = exx * exx + eyy * eyy + ezz * ezz + 2.0 * (exy * exy + exz * exz + eyz * eyz)
            density = SHEAR * square + 0.5 * LAME * trace * trace

            @pl.when(load == 0)
            def _():
                out_ref[p, :, cols] = density

            @pl.when(load > 0)
            def _():
                out_ref[p, :, cols] = out_ref[p, :, cols] + density

    @pl.when(load == pl.num_programs(0) - 1)
    def _():
        peak_ref[...] = jnp.zeros(peak_ref.shape, jnp.float32)

        @pl.loop(0, size_x)
        def _(p):
            energy = stiff_ref[p] * out_ref[p]
            out_ref[p] = energy
            peak_ref[...] = jnp.maximum(peak_ref[...], energy)


def slab_energy(displacement, material):
    loads, comps, size_x, size_y, size_z = displacement.shape
    low_y = shift_from(displacement, "narrow", 3, 1, True)
    high_y = shift_from(displacement, "narrow", 3, 2, False)
    filler = jnp.zeros((loads, comps, size_x, 5, size_z), jnp.float32)
    tail = jnp.concatenate([high_y, filler, low_y], axis=3)
    ends = jnp.concatenate(
        [
            jnp.concatenate([displacement[:, :, :2], displacement[:, :, -1:]], axis=2),
            jnp.concatenate([tail[:, :, :2], tail[:, :, -1:]], axis=2),
        ],
        axis=3,
    )
    high_x = shift_from(ends, "wide", 2, 2, False)
    low_x = shift_from(ends, "wide", 2, 1, True)
    beside = jnp.concatenate([high_x, low_x], axis=2)
    beside_own = beside[:, :, :, :size_y]
    tail = jnp.concatenate([tail, beside[:, :, :, size_y:]], axis=2)
    stiffness = 0.2 + 0.8 * jnp.repeat(material.astype(jnp.float32), BZ, axis=2)
    planes = size_x + 3
    rows = size_y + 8
    energy, peak = pl.pallas_call(
        energy_kernel,
        grid=(loads,),
        out_shape=(
            jax.ShapeDtypeStruct((size_x, size_y, size_z), jnp.float32),
            jax.ShapeDtypeStruct((size_y, size_z), jnp.float32),
        ),
        in_specs=[
            pl.BlockSpec((1, comps, size_x, size_y, size_z), lambda i: (i, 0, 0, 0, 0)),
            pl.BlockSpec((1, comps, 3, size_y, size_z), lambda i: (i, 0, 0, 0, 0)),
            pl.BlockSpec((1, comps, planes, 8, size_z), lambda i: (i, 0, 0, 0, 0)),
            pl.BlockSpec((size_x, size_y, size_z), lambda i: (0, 0, 0)),
        ],
        out_specs=(
            pl.BlockSpec((size_x, size_y, size_z), lambda i: (0, 0, 0)),
            pl.BlockSpec((size_y, size_z), lambda i: (0, 0)),
        ),
        scratch_shapes=[
            pltpu.VMEM((comps, planes, rows, size_z), jnp.float32),
            pltpu.VMEM((comps, planes, rows, size_z), jnp.float32),
        ],
        compiler_params=pltpu.CompilerParams(vmem_limit_bytes=40 << 20),
        cost_estimate=pl.CostEstimate(flops=100000000, bytes_accessed=12000000, transcendentals=0),
    )(displacement, beside_own, tail, stiffness)
    return energy, jnp.max(peak)


def neighbour_mean(padded):
    wider = jnp.pad(padded, ((0, 0), (0, 0), (1, 1)))
    total = wider[2:, 1:-1, 1:-1] + wider[:-2, 1:-1, 1:-1]
    total = total + wider[1:-1, 2:, 1:-1] + wider[1:-1, :-2, 1:-1]
    total = total + wider[1:-1, 1:-1, 2:] + wider[1:-1, 1:-1, :-2]
    return total * (1.0 / 6.0)


def weno_side(v1, v2, v3, v4, v5):
    p_one = v1 / 3.0 - 7.0 * v2 / 6.0 + 11.0 * v3 / 6.0
    p_two = -v2 / 6.0 + 5.0 * v3 / 6.0 + v4 / 3.0
    p_three = v3 / 3.0 + 5.0 * v4 / 6.0 - v5 / 6.0
    b_one = 13.0 / 12.0 * (v1 - 2.0 * v2 + v3) ** 2 + 0.25 * (v1 - 4.0 * v2 + 3.0 * v3) ** 2
    b_two = 13.0 / 12.0 * (v2 - 2.0 * v3 + v4) ** 2 + 0.25 * (v2 - v4) ** 2
    b_three = 13.0 / 12.0 * (v3 - 2.0 * v4 + v5) ** 2 + 0.25 * (3.0 * v3 - 4.0 * v4 + v5) ** 2
    a_one = 0.1 / (WENO_EPS + b_one) ** 2
    a_two = 0.6 / (WENO_EPS + b_two) ** 2
    a_three = 0.3 / (WENO_EPS + b_three) ** 2
    return (a_one * p_one + a_two * p_two + a_three * p_three) / (a_one + a_two + a_three)


def march_step(padded, speed):
    wider = jnp.pad(padded, ((0, 0), (0, 0), (3, 3)), constant_values=1.0)
    size_z = padded.shape[0] - 6
    size_y = padded.shape[1] - 6
    size_x = padded.shape[2]
    centre = wider[3 : 3 + size_z, 3 : 3 + size_y, 3 : 3 + size_x]
    lines = (
        wider[:, 3 : 3 + size_y, 3 : 3 + size_x],
        wider[3 : 3 + size_z, :, 3 : 3 + size_x],
        wider[3 : 3 + size_z, 3 : 3 + size_y, :],
    )
    grow_plus = None
    grow_minus = None
    for axis in range(3):
        line = lines[axis]
        count = centre.shape[axis]
        diffs = lax.slice_in_dim(line, 1, count + 6, axis=axis) - lax.slice_in_dim(
            line, 0, count + 5, axis=axis
        )
        parts = [lax.slice_in_dim(diffs, k, k + count, axis=axis) for k in range(6)]
        minus = weno_side(parts[0], parts[1], parts[2], parts[3], parts[4])
        plus = weno_side(parts[5], parts[4], parts[3], parts[2], parts[1])
        term_p = jnp.maximum(jnp.maximum(minus, 0.0) ** 2, jnp.minimum(plus, 0.0) ** 2)
        term_m = jnp.maximum(jnp.minimum(minus, 0.0) ** 2, jnp.maximum(plus, 0.0) ** 2)
        grow_plus = term_p if grow_plus is None else grow_plus + term_p
        grow_minus = term_m if grow_minus is None else grow_minus + term_m
    return centre - TIME_STEP * (
        jnp.maximum(speed, 0.0) * jnp.sqrt(grow_plus)
        + jnp.minimum(speed, 0.0) * jnp.sqrt(grow_minus)
    )


def inner_region(array, margin):
    return array[margin : array.shape[0] - margin, margin : array.shape[1] - margin]


def ghost_fill(array, margin, value):
    own_z = array.shape[0] - 2 * margin
    own_y = array.shape[1] - 2 * margin
    pos_z = lax.axis_index("wide") * own_z - margin + jnp.arange(array.shape[0], dtype=jnp.int32)
    pos_y = lax.axis_index("narrow") * own_y - margin + jnp.arange(array.shape[1], dtype=jnp.int32)
    valid_z = (pos_z >= 0) & (pos_z < own_z * lax.axis_size("wide"))
    valid_y = (pos_y >= 0) & (pos_y < own_y * lax.axis_size("narrow"))
    inside = valid_z[:, None, None] & valid_y[None, :, None]
    return jnp.where(inside, array, value)


def per_device(displacement, material, level_set):
    energy, own_peak = slab_energy(displacement, material)
    devices = lax.axis_size("wide") * lax.axis_size("narrow")
    peaks = lax.all_to_all(
        jnp.full((devices, 1, 128), own_peak), ("wide", "narrow"), split_axis=0, concat_axis=0, tiled=True
    )
    moved = lax.all_to_all(
        jnp.transpose(energy, (2, 1, 0)), "wide", split_axis=0, concat_axis=2, tiled=True
    )
    velocity = moved / (jnp.max(peaks) + 1e-06) - 0.5
    vel_wide, phi_wide = (
        with_halo(velocity, (("wide", 0), ("narrow", 1)), EXT_PASSES),
        with_halo(level_set, (("wide", 0), ("narrow", 1)), EXT_PASSES),
    )
    weight_wide = 1.0 / (1.0 + 4.0 * phi_wide * phi_wide)
    speed = vel_wide
    for step in range(EXT_PASSES):
        speed = ghost_fill(speed, EXT_PASSES - step, 0.0)
        weight_in = inner_region(weight_wide, step + 1)
        speed = weight_in * inner_region(vel_wide, step + 1) + (1.0 - weight_in) * neighbour_mean(
            speed
        )
    phi = level_set
    for step in range(HJ_STEPS):
        beside_all = with_halo(phi, (("wide", 0), ("narrow", 1)), 3)
        phi = march_step(ghost_fill(beside_all, 3, 1.0), speed)
    return (phi, speed)


def solution(mesh):
    return jax.shard_map(
        per_device,
        mesh=mesh,
        in_specs=(
            P(None, None, "wide", "narrow", None),
            P("wide", "narrow", None),
            P("wide", "narrow", None),
        ),
        out_specs=(P("wide", "narrow", None), P("wide", "narrow", None)),
        check_vma=False,
    )
```

```python
import functools

import jax
import jax.numpy as jnp
from jax import lax
from jax.experimental import pallas as pl
from jax.experimental.pallas import tpu as pltpu
from jax.sharding import PartitionSpec as P

BZ = 16
EXT_PASSES = 4
HJ_STEPS = 3


SHEAR = 0.384615
LAME = 0.576923
WENO_EPS = 1e-06
TIME_STEP = 0.3
VAL_TAPS = (1.0 / 48.0, 23.0 / 48.0, 23.0 / 48.0, 1.0 / 48.0)
DER_TAPS = (-1.0 / 8.0, -5.0 / 8.0, 5.0 / 8.0, 1.0 / 8.0)


def shift_from(block, axis, dim, width, up):
    count = lax.axis_size(axis)
    if up:
        pairs = [(i, i + 1) for i in range(count - 1)]
        part = lax.slice_in_dim(block, block.shape[dim] - width, None, axis=dim)
    else:
        pairs = [(i + 1, i) for i in range(count - 1)]
        part = lax.slice_in_dim(block, 0, width, axis=dim)
    return lax.ppermute(part, axis, pairs)


def z_filters(u):
    size = u.shape[-1]
    lane = lax.broadcasted_iota(jnp.int32, u.shape, u.ndim - 1)
    last = u.ndim - 1
    before = jnp.where(lane == 0, 0.0, pltpu.roll(u, 1, last))
    after = jnp.where(lane == size - 1, 0.0, pltpu.roll(u, size - 1, last))
    second = jnp.where(lane >= size - 2, 0.0, pltpu.roll(u, size - 2, last))
    val = VAL_TAPS[0] * (before + second) + VAL_TAPS[1] * (u + after)
    der = DER_TAPS[3] * (second - before) + DER_TAPS[2] * (after - u)
    return val, der


def energy_kernel(own_ref, xh_ref, yh_ref, stiff_ref, out_ref, peak_ref, val_ref, der_ref):
    load = pl.program_id(0)
    size_x, size_y, size_z = own_ref.shape[2:]
    rows = val_ref.shape[2]

    def plane(c, p, body, tail):
        val, der = z_filters(body)
        val_ref[c, p, 0:size_y, :] = val
        der_ref[c, p, 0:size_y, :] = der
        val, der = z_filters(tail)
        val_ref[c, p, size_y:rows, :] = val
        der_ref[c, p, size_y:rows, :] = der

    for c in range(3):
        @pl.loop(0, size_x)
        def _(p):
            plane(c, p, own_ref[0, c, p], yh_ref[0, c, p])

        @pl.loop(0, 3)
        def _(q):
            plane(c, size_x + q, xh_ref[0, c, q], yh_ref[0, c, size_x + q])

    def taps_x(ref, c, idx, cols):
        parts = [ref[c, i, :, cols] for i in idx]
        return parts[0] + parts[3], parts[1] + parts[2], parts[3] - parts[0], parts[2] - parts[1]

    def along_y(val_part, der_part):
        total = None
        for k, shift in enumerate((1, 0, rows - 1, rows - 2)):
            term = None
            if val_part is not None:
                term = VAL_TAPS[k] * val_part
            if der_part is not None:
                extra = DER_TAPS[k] * der_part
                term = extra if term is None else term + extra
            if shift:
                term = pltpu.roll(term, shift, 0)
            total = term if total is None else total + term
        return total[0:size_y]

    chunk = 128

    @pl.loop(0, size_x)
    def _(p):
        low = jnp.where(p == 0, size_x + 2, p - 1)
        idx = (low, p, p + 1, p + 2)
        for piece in range(size_z // chunk):
            cols = pl.ds(piece * chunk, chunk)
            fields = []
            for c in range(3):
                outer, inner, far, near = taps_x(val_ref, c, idx, cols)
                vv = VAL_TAPS[0] * outer + VAL_TAPS[1] * inner
                dv = DER_TAPS[3] * far + DER_TAPS[2] * near
                outer, inner, _, _ = taps_x(der_ref, c, idx, cols)
                vz = VAL_TAPS[0] * outer + VAL_TAPS[1] * inner
                fields.append((vv, dv, vz))
            exx = along_y(fields[0][1], None)
            eyy = along_y(None, fields[1][0])
            ezz = along_y(fields[2][2], None)
            exy = 0.5 * along_y(fields[1][1], fields[0][0])
            exz = 0.5 * along_y(fields[0][2] + fields[2][1], None)
            eyz = 0.5 * along_y(fields[1][2], fields[2][0])
            trace = exx + eyy + ezz
            square = exx * exx + eyy * eyy + ezz * ezz + 2.0 * (exy * exy + exz * exz + eyz * eyz)
            density = SHEAR * square + 0.5 * LAME * trace * trace

            @pl.when(load == 0)
            def _():
                out_ref[p, :, cols] = density

            @pl.when(load > 0)
            def _():
                out_ref[p, :, cols] = out_ref[p, :, cols] + density

    @pl.when(load == pl.num_programs(0) - 1)
    def _():
        peak_ref[...] = jnp.zeros(peak_ref.shape, jnp.float32)

        @pl.loop(0, size_x)
        def _(p):
            energy = stiff_ref[p] * out_ref[p]
            out_ref[p] = energy
            peak_ref[...] = jnp.maximum(peak_ref[...], energy)


def slab_energy(displacement, material, early):
    loads, comps, size_x, size_y, size_z = displacement.shape
    low_y = shift_from(displacement, "narrow", 3, 1, True)
    high_y = shift_from(displacement, "narrow", 3, 2, False)
    filler = jnp.zeros((loads, comps, size_x, 5, size_z), jnp.float32)
    tail = jnp.concatenate([high_y, filler, low_y], axis=3)
    ends = jnp.concatenate(
        [
            jnp.concatenate([displacement[:, :, :2], displacement[:, :, -1:]], axis=2),
            jnp.concatenate([tail[:, :, :2], tail[:, :, -1:]], axis=2),
        ],
        axis=3,
    )
    high_x = shift_from(ends, "wide", 2, 2, False)
    low_x = shift_from(ends, "wide", 2, 1, True)
    beside = jnp.concatenate([high_x, low_x], axis=2)
    beside_own = beside[:, :, :, :size_y]
    tail = jnp.concatenate([tail, beside[:, :, :, size_y:]], axis=2)
    stiffness = 0.2 + 0.8 * jnp.repeat(material.astype(jnp.float32), BZ, axis=2)
    beside_own, tail, early = lax.optimization_barrier((beside_own, tail, early))
    planes = size_x + 3
    rows = size_y + 8
    energy, peak = pl.pallas_call(
        energy_kernel,
        grid=(loads,),
        out_shape=(
            jax.ShapeDtypeStruct((size_x, size_y, size_z), jnp.float32),
            jax.ShapeDtypeStruct((size_y, size_z), jnp.float32),
        ),
        in_specs=[
            pl.BlockSpec((1, comps, size_x, size_y, size_z), lambda i: (i, 0, 0, 0, 0)),
            pl.BlockSpec((1, comps, 3, size_y, size_z), lambda i: (i, 0, 0, 0, 0)),
            pl.BlockSpec((1, comps, planes, 8, size_z), lambda i: (i, 0, 0, 0, 0)),
            pl.BlockSpec((size_x, size_y, size_z), lambda i: (0, 0, 0)),
        ],
        out_specs=(
            pl.BlockSpec((size_x, size_y, size_z), lambda i: (0, 0, 0)),
            pl.BlockSpec((size_y, size_z), lambda i: (0, 0)),
        ),
        scratch_shapes=[
            pltpu.VMEM((comps, planes, rows, size_z), jnp.float32),
            pltpu.VMEM((comps, planes, rows, size_z), jnp.float32),
        ],
        compiler_params=pltpu.CompilerParams(vmem_limit_bytes=40 << 20),
        cost_estimate=pl.CostEstimate(flops=100000000, bytes_accessed=12000000, transcendentals=0),
    )(displacement, beside_own, tail, stiffness)
    return energy, jnp.max(peak), early


def weno_pair(d):
    e = [d[k + 1] - d[k] for k in range(5)]
    s = [e[k + 1] - e[k] for k in range(4)]
    bend = [(13.0 / 12.0) * s[k] * s[k] for k in range(4)]
    twice = [None] + [2.0 * e[k] for k in (1, 2, 3)]
    sixth = [None] + [(1.0 / 6.0) * e[k] for k in (1, 2, 3)]
    third = (1.0 / 3.0) * e[2]

    def blend(base, b_one, t_one, b_two, t_two, b_three, t_three, r_one, r_two, r_three):
        a = WENO_EPS + b_one + 0.25 * t_one * t_one
        b = WENO_EPS + b_two + 0.25 * t_two * t_two
        c = WENO_EPS + b_three + 0.25 * t_three * t_three
        a = a * a
        b = b * b
        c = c * c
        w_one = 0.1 * (b * c)
        w_two = 0.6 * (a * c)
        w_three = 0.3 * (a * b)
        return base + (w_one * r_one + w_two * r_two + w_three * r_three) / (w_one + w_two + w_three)

    minus = blend(
        d[2],
        bend[0], s[0] + twice[1],
        bend[1], e[1] + e[2],
        bend[2], s[2] - twice[2],
        (5.0 / 6.0) * e[1] - (1.0 / 3.0) * e[0],
        sixth[1] + third,
        2.0 * third - sixth[3],
    )
    plus = blend(
        d[3],
        bend[3], s[3] - twice[3],
        bend[2], e[2] + e[3],
        bend[1], s[1] + twice[2],
        (1.0 / 3.0) * e[4] - (5.0 / 6.0) * e[3],
        -(sixth[3] + third),
        sixth[1] - 2.0 * third,
    )
    return minus, plus


def lane_shift(u, offset, ghost):
    if offset == 0:
        return u
    size = u.shape[-1]
    lane = lax.broadcasted_iota(jnp.int32, u.shape, u.ndim - 1)
    moved = pltpu.roll(u, (-offset) % size, u.ndim - 1)
    outside = lane >= size - offset if offset > 0 else lane < -offset
    return jnp.where(outside, ghost, moved)


MARGIN = 3 * (HJ_STEPS - 1) + EXT_PASSES
SIDE = -(-MARGIN // 8) * 8 + 8


CHUNK = 8


def march_kernel(
    place, peak, vel_own, vel_low, vel_high, phi_own, phi_low, phi_high,
    next_ref, speed_ref, pull, keep, one, two, first, second,
):
    deep, rows, size_x = pull.shape
    own_y = rows - 2 * SIDE
    own_z = deep - 2 * MARGIN
    scale = peak[0] + 1e-06

    def settle(z, lo, values, ghost):
        here = place[0] + z
        shape = values.shape
        row = lax.broadcasted_iota(jnp.int32, shape, 0) + (lo + place[2])
        lowest = jnp.where((here >= 0) & (here < place[1]), 0, place[3])
        return jnp.where((row >= lowest) & (row < place[3]), values, ghost)

    def window(margin):
        lo = (SIDE - margin) // 8 * 8
        return lo, rows - lo

    @pl.loop(0, deep)
    def _(z):
        def fill(lo, size, energy, phi):
            at = pl.ds(lo, size)
            velocity = energy / scale - 0.5
            weight = 1.0 / (1.0 + 4.0 * phi * phi)
            pull[z, at, :] = weight * velocity
            keep[z, at, :] = (1.0 - weight) * (1.0 / 6.0)
            one[z, at, :] = settle(z, lo, velocity, 0.0)
            first[z, at, :] = settle(z, lo, phi, 1.0)

        fill(SIDE - MARGIN, MARGIN, vel_low[z], phi_low[z])
        fill(SIDE, own_y, vel_own[z], phi_own[z])
        fill(SIDE + own_y, MARGIN, vel_high[z], phi_high[z])

    source, target = one, two
    for step in range(EXT_PASSES):
        margin = MARGIN - 1 - step
        lo, hi = window(margin)

        def extend(z, source=source, target=target, lo=lo, hi=hi):
            for start in range(lo, hi, 16):
                at = pl.ds(start, 16)
                mid = source[z, at, :]
                total = source[z - 1, at, :] + source[z + 1, at, :]
                total = total + (source[z, pl.ds(start - 1, 16), :] + source[z, pl.ds(start + 1, 16), :])
                total = total + (lane_shift(mid, 1, 0.0) + lane_shift(mid, -1, 0.0))
                value = pull[z, at, :] + keep[z, at, :] * total
                target[z, at, :] = settle(z, start, value, 0.0)

        pl.loop(step + 1, deep - step - 1)(extend)
        source, target = target, source
    speed = source

    source, target = first, second
    for step in range(HJ_STEPS):
        margin = 3 * (HJ_STEPS - 1 - step)
        lo, hi = window(margin)
        final = step == HJ_STEPS - 1

        def march(z, source=source, target=target, lo=lo, hi=hi, final=final):
            for start in range(lo, hi, CHUNK):
                at = pl.ds(start, CHUNK)
                mid = source[z, at, :]
                lines = (
                    [source[z + k, at, :] for k in range(-3, 4)],
                    [source[z, pl.ds(start + k, CHUNK), :] for k in range(-3, 4)],
                    [lane_shift(mid, k, 1.0) for k in range(-3, 4)],
                )
                grow_plus = None
                grow_minus = None
                for line in lines:
                    minus, plus = weno_pair([line[k + 1] - line[k] for k in range(6)])
                    up = jnp.maximum(jnp.maximum(minus, 0.0), -jnp.minimum(plus, 0.0))
                    down = jnp.maximum(-jnp.minimum(minus, 0.0), jnp.maximum(plus, 0.0))
                    grow_plus = up * up if grow_plus is None else grow_plus + up * up
                    grow_minus = down * down if grow_minus is None else grow_minus + down * down
                rate = speed[z, at, :]
                growth = jnp.sqrt(jnp.where(rate > 0.0, grow_plus, grow_minus))
                value = mid - TIME_STEP * (rate * growth)
                if final:
                    next_ref[z - MARGIN, pl.ds(start - SIDE, CHUNK), :] = value
                    speed_ref[z - MARGIN, pl.ds(start - SIDE, CHUNK), :] = rate
                else:
                    target[z, at, :] = settle(z, start, value, 1.0)

        pl.loop(MARGIN - margin, MARGIN + own_z + margin)(march)
        source, target = target, source


def rows_beside(block, width):
    low = shift_from(block, "narrow", 1, width, True)
    high = shift_from(block, "narrow", 1, width, False)
    return block, low, high


def march(velocity, phi, peak, own_z, own_y):
    deep, _, size_x = phi[0].shape
    place = jnp.stack(
        [
            lax.axis_index("wide") * own_z - MARGIN,
            lax.axis_size("wide") * own_z,
            lax.axis_index("narrow") * own_y - SIDE,
            lax.axis_size("narrow") * own_y,
        ]
    ).astype(jnp.int32)
    result = jax.ShapeDtypeStruct((own_z, own_y, size_x), jnp.float32)
    smem = pl.BlockSpec(memory_space=pltpu.SMEM)
    vmem = pl.BlockSpec(memory_space=pltpu.VMEM)
    return pl.pallas_call(
        march_kernel,
        out_shape=(result, result),
        in_specs=[smem, smem] + [vmem] * 6,
        out_specs=(vmem, vmem),
        scratch_shapes=[pltpu.VMEM((deep, own_y + 2 * SIDE, size_x), jnp.float32)] * 6,
        compiler_params=pltpu.CompilerParams(vmem_limit_bytes=56 << 20),
        cost_estimate=pl.CostEstimate(flops=200000000, bytes_accessed=8000000, transcendentals=0),
    )(place, jnp.reshape(peak, (1,)), *velocity, *phi)


def per_device(displacement, material, level_set):
    own_z, own_y, size_x = level_set.shape
    low = shift_from(level_set, "wide", 0, MARGIN, True)
    high = shift_from(level_set, "wide", 0, MARGIN, False)
    phi = rows_beside(jnp.concatenate([low, level_set, high], axis=0), MARGIN)
    energy, own_peak, phi = slab_energy(displacement, material, phi)
    devices = lax.axis_size("wide") * lax.axis_size("narrow")
    peaks = lax.all_to_all(
        jnp.full((devices, 1, 128), own_peak), ("wide", "narrow"), split_axis=0, concat_axis=0, tiled=True
    )
    flipped = jnp.pad(jnp.transpose(energy, (2, 1, 0)), ((MARGIN, MARGIN), (0, 0), (0, 0)))
    chunks = [
        lax.slice_in_dim(flipped, k * own_z, k * own_z + own_z + 2 * MARGIN, axis=0)
        for k in range(lax.axis_size("wide"))
    ]
    moved = lax.all_to_all(
        jnp.concatenate(chunks, axis=0), "wide", split_axis=0, concat_axis=2, tiled=True
    )
    return march(rows_beside(moved, MARGIN), phi, jnp.max(peaks), own_z, own_y)


def solution(mesh):
    return jax.shard_map(
        per_device,
        mesh=mesh,
        in_specs=(
            P(None, None, "wide", "narrow", None),
            P("wide", "narrow", None),
            P("wide", "narrow", None),
        ),
        out_specs=(P("wide", "narrow", None), P("wide", "narrow", None)),
        check_vma=False,
    )
```

```python
import functools

import jax
import jax.numpy as jnp
from jax import lax
from jax.experimental import pallas as pl
from jax.experimental.pallas import tpu as pltpu
from jax.sharding import PartitionSpec as P

BZ = 16
EXT_PASSES = 4
HJ_STEPS = 3


SHEAR = 0.384615
LAME = 0.576923
WENO_EPS = 1e-06
TIME_STEP = 0.3
VAL_TAPS = (1.0 / 48.0, 23.0 / 48.0, 23.0 / 48.0, 1.0 / 48.0)
DER_TAPS = (-1.0 / 8.0, -5.0 / 8.0, 5.0 / 8.0, 1.0 / 8.0)


def shift_from(block, axis, dim, width, up):
    count = lax.axis_size(axis)
    if up:
        pairs = [(i, i + 1) for i in range(count - 1)]
        part = lax.slice_in_dim(block, block.shape[dim] - width, None, axis=dim)
    else:
        pairs = [(i + 1, i) for i in range(count - 1)]
        part = lax.slice_in_dim(block, 0, width, axis=dim)
    return lax.ppermute(part, axis, pairs)


def z_filters(u):
    size = u.shape[-1]
    lane = lax.broadcasted_iota(jnp.int32, u.shape, u.ndim - 1)
    last = u.ndim - 1
    before = jnp.where(lane == 0, 0.0, pltpu.roll(u, 1, last))
    after = jnp.where(lane == size - 1, 0.0, pltpu.roll(u, size - 1, last))
    second = jnp.where(lane >= size - 2, 0.0, pltpu.roll(u, size - 2, last))
    val = VAL_TAPS[0] * (before + second) + VAL_TAPS[1] * (u + after)
    der = DER_TAPS[3] * (second - before) + DER_TAPS[2] * (after - u)
    return val, der


def energy_kernel(jump, own_ref, yh_ref, stiff_ref, out_ref, peak_ref, val_ref, der_ref):
    load = pl.program_id(0)
    planes, size_y, size_z = own_ref.shape[2:]
    made = out_ref.shape[0]
    rows = val_ref.shape[2]

    def plane(c, p, body, tail):
        val, der = z_filters(body)
        val_ref[c, p, 0:size_y, :] = val
        der_ref[c, p, 0:size_y, :] = der
        val, der = z_filters(tail)
        val_ref[c, p, size_y:rows, :] = val
        der_ref[c, p, size_y:rows, :] = der

    for c in range(3):
        @pl.loop(0, planes)
        def _(p):
            plane(c, p, own_ref[0, c, p], yh_ref[0, c, p])

    def taps_x(ref, c, idx, cols):
        parts = [ref[c, i, :, cols] for i in idx]
        return parts[0] + parts[3], parts[1] + parts[2], parts[3] - parts[0], parts[2] - parts[1]

    def along_y(val_part, der_part):
        total = None
        for k, shift in enumerate((1, 0, rows - 1, rows - 2)):
            term = None
            if val_part is not None:
                term = VAL_TAPS[k] * val_part
            if der_part is not None:
                extra = DER_TAPS[k] * der_part
                term = extra if term is None else term + extra
            if shift:
                term = pltpu.roll(term, shift, 0)
            total = term if total is None else total + term
        return total[0:size_y]

    chunk = 128

    @pl.loop(0, made)
    def _(p):
        base = jnp.where(p == 0, 0, p + jump) if jump else p
        idx = (base, base + 1, base + 2, base + 3)
        for piece in range(size_z // chunk):
            cols = pl.ds(piece * chunk, chunk)
            fields = []
            for c in range(3):
                outer, inner, far, near = taps_x(val_ref, c, idx, cols)
                vv = VAL_TAPS[0] * outer + VAL_TAPS[1] * inner
                dv = DER_TAPS[3] * far + DER_TAPS[2] * near
                outer, inner, _, _ = taps_x(der_ref, c, idx, cols)
                vz = VAL_TAPS[0] * outer + VAL_TAPS[1] * inner
                fields.append((vv, dv, vz))
            exx = along_y(fields[0][1], None)
            eyy = along_y(None, fields[1][0])
            ezz = along_y(fields[2][2], None)
            exy = 0.5 * along_y(fields[1][1], fields[0][0])
            exz = 0.5 * along_y(fields[0][2] + fields[2][1], None)
            eyz = 0.5 * along_y(fields[1][2], fields[2][0])
            trace = exx + eyy + ezz
            square = exx * exx + eyy * eyy + ezz * ezz + 2.0 * (exy * exy + exz * exz + eyz * eyz)
            density = SHEAR * square + 0.5 * LAME * trace * trace

            @pl.when(load == 0)
            def _():
                out_ref[p, :, cols] = density

            @pl.when(load > 0)
            def _():
                out_ref[p, :, cols] = out_ref[p, :, cols] + density

    @pl.when(load == pl.num_programs(0) - 1)
    def _():
        peak_ref[...] = jnp.zeros(peak_ref.shape, jnp.float32)

        @pl.loop(0, made)
        def _(p):
            energy = stiff_ref[p] * out_ref[p]
            out_ref[p] = energy
            peak_ref[...] = jnp.maximum(peak_ref[...], energy)


def energy_of(planes, tail, stiffness, jump):
    loads, comps, count, size_y, size_z = planes.shape
    made = stiffness.shape[0]
    return pl.pallas_call(
        functools.partial(energy_kernel, jump),
        grid=(loads,),
        out_shape=(
            jax.ShapeDtypeStruct((made, size_y, size_z), jnp.float32),
            jax.ShapeDtypeStruct((size_y, size_z), jnp.float32),
        ),
        in_specs=[
            pl.BlockSpec((1, comps, count, size_y, size_z), lambda i: (i, 0, 0, 0, 0)),
            pl.BlockSpec((1, comps, count, 8, size_z), lambda i: (i, 0, 0, 0, 0)),
            pl.BlockSpec((made, size_y, size_z), lambda i: (0, 0, 0)),
        ],
        out_specs=(
            pl.BlockSpec((made, size_y, size_z), lambda i: (0, 0, 0)),
            pl.BlockSpec((size_y, size_z), lambda i: (0, 0)),
        ),
        scratch_shapes=[pltpu.VMEM((comps, count, size_y + 8, size_z), jnp.float32)] * 2,
        compiler_params=pltpu.CompilerParams(vmem_limit_bytes=40 << 20),
        cost_estimate=pl.CostEstimate(
            flops=6000000 * made, bytes_accessed=6000000 * made, transcendentals=0
        ),
    )(planes, tail, stiffness)


def slab_energy(displacement, material, early):
    loads, comps, size_x, size_y, size_z = displacement.shape
    high_x = shift_from(displacement, "wide", 2, 2, False)
    low_x = shift_from(displacement, "wide", 2, 1, True)
    low_y = shift_from(displacement, "narrow", 3, 1, True)
    high_y = shift_from(displacement, "narrow", 3, 2, False)
    filler = jnp.zeros((loads, comps, size_x, 5, size_z), jnp.float32)
    tail = jnp.concatenate([high_y, filler, low_y], axis=3)
    high_tail = shift_from(tail, "wide", 2, 2, False)
    low_tail = shift_from(tail, "wide", 2, 1, True)
    stiffness = 0.2 + 0.8 * jnp.repeat(material.astype(jnp.float32), BZ, axis=2)
    inner, inner_peak = energy_of(displacement, tail, stiffness[1 : size_x - 2], 0)

    def edges(block, low, high):
        return jnp.concatenate([low, block[:, :, :3], block[:, :, size_x - 3 :], high], axis=2)

    beside, beside_tail, early = lax.optimization_barrier(
        (edges(displacement, low_x, high_x), edges(tail, low_tail, high_tail), early)
    )
    rim, rim_peak = energy_of(
        beside, beside_tail, jnp.concatenate([stiffness[:1], stiffness[size_x - 2 :]], axis=0), 3
    )
    energy = jnp.concatenate([rim[:1], inner, rim[1:]], axis=0)
    return energy, jnp.max(jnp.maximum(inner_peak, rim_peak)), early


def weno_pair(d):
    e = [d[k + 1] - d[k] for k in range(5)]
    s = [e[k + 1] - e[k] for k in range(4)]
    bend = [(13.0 / 12.0) * s[k] * s[k] for k in range(4)]
    twice = [None] + [2.0 * e[k] for k in (1, 2, 3)]
    sixth = [None] + [(1.0 / 6.0) * e[k] for k in (1, 2, 3)]
    third = (1.0 / 3.0) * e[2]

    def blend(base, b_one, t_one, b_two, t_two, b_three, t_three, r_one, r_two, r_three):
        a = WENO_EPS + b_one + 0.25 * t_one * t_one
        b = WENO_EPS + b_two + 0.25 * t_two * t_two
        c = WENO_EPS + b_three + 0.25 * t_three * t_three
        a = a * a
        b = b * b
        c = c * c
        w_one = 0.1 * (b * c)
        w_two = 0.6 * (a * c)
        w_three = 0.3 * (a * b)
        return base + (w_one * r_one + w_two * r_two + w_three * r_three) / (w_one + w_two + w_three)

    minus = blend(
        d[2],
        bend[0], s[0] + twice[1],
        bend[1], e[1] + e[2],
        bend[2], s[2] - twice[2],
        (5.0 / 6.0) * e[1] - (1.0 / 3.0) * e[0],
        sixth[1] + third,
        2.0 * third - sixth[3],
    )
    plus = blend(
        d[3],
        bend[3], s[3] - twice[3],
        bend[2], e[2] + e[3],
        bend[1], s[1] + twice[2],
        (1.0 / 3.0) * e[4] - (5.0 / 6.0) * e[3],
        -(sixth[3] + third),
        sixth[1] - 2.0 * third,
    )
    return minus, plus


def lane_shift(u, offset, ghost):
    if offset == 0:
        return u
    size = u.shape[-1]
    lane = lax.broadcasted_iota(jnp.int32, u.shape, u.ndim - 1)
    moved = pltpu.roll(u, (-offset) % size, u.ndim - 1)
    outside = lane >= size - offset if offset > 0 else lane < -offset
    return jnp.where(outside, ghost, moved)


MARGIN = 3 * (HJ_STEPS - 1) + EXT_PASSES
SIDE = -(-MARGIN // 8) * 8 + 8


CHUNK = 8


def march_kernel(
    place, peak, vel_own, vel_low, vel_high, phi_own, phi_low, phi_high,
    next_ref, speed_ref, pull, keep, one, two, first, second,
):
    deep, rows, size_x = pull.shape
    own_y = rows - 2 * SIDE
    own_z = deep - 2 * MARGIN
    scale = peak[0] + 1e-06

    def settle(z, lo, values, ghost):
        here = place[0] + z
        shape = values.shape
        row = lax.broadcasted_iota(jnp.int32, shape, 0) + (lo + place[2])
        lowest = jnp.where((here >= 0) & (here < place[1]), 0, place[3])
        return jnp.where((row >= lowest) & (row < place[3]), values, ghost)

    def window(margin):
        lo = (SIDE - margin) // 8 * 8
        return lo, rows - lo

    @pl.loop(0, deep)
    def _(z):
        def fill(lo, size, energy, phi):
            at = pl.ds(lo, size)
            velocity = energy / scale - 0.5
            weight = 1.0 / (1.0 + 4.0 * phi * phi)
            pull[z, at, :] = weight * velocity
            keep[z, at, :] = (1.0 - weight) * (1.0 / 6.0)
            one[z, at, :] = settle(z, lo, velocity, 0.0)
            first[z, at, :] = settle(z, lo, phi, 1.0)

        fill(SIDE - MARGIN, MARGIN, vel_low[z], phi_low[z])
        fill(SIDE, own_y, vel_own[z], phi_own[z])
        fill(SIDE + own_y, MARGIN, vel_high[z], phi_high[z])

    source, target = one, two
    for step in range(EXT_PASSES):
        margin = MARGIN - 1 - step
        lo, hi = window(margin)

        def extend(z, source=source, target=target, lo=lo, hi=hi):
            for start in range(lo, hi, 16):
                at = pl.ds(start, 16)
                mid = source[z, at, :]
                total = source[z - 1, at, :] + source[z + 1, at, :]
                total = total + (source[z, pl.ds(start - 1, 16), :] + source[z, pl.ds(start + 1, 16), :])
                total = total + (lane_shift(mid, 1, 0.0) + lane_shift(mid, -1, 0.0))
                value = pull[z, at, :] + keep[z, at, :] * total
                target[z, at, :] = settle(z, start, value, 0.0)

        pl.loop(step + 1, deep - step - 1)(extend)
        source, target = target, source
    speed = source

    source, target = first, second
    for step in range(HJ_STEPS):
        margin = 3 * (HJ_STEPS - 1 - step)
        lo, hi = window(margin)
        final = step == HJ_STEPS - 1

        def march(z, source=source, target=target, lo=lo, hi=hi, final=final):
            for start in range(lo, hi, CHUNK):
                at = pl.ds(start, CHUNK)
                mid = source[z, at, :]
                lines = (
                    [source[z + k, at, :] for k in range(-3, 4)],
                    [source[z, pl.ds(start + k, CHUNK), :] for k in range(-3, 4)],
                    [lane_shift(mid, k, 1.0) for k in range(-3, 4)],
                )
                grow_plus = None
                grow_minus = None
                for line in lines:
                    minus, plus = weno_pair([line[k + 1] - line[k] for k in range(6)])
                    up = jnp.maximum(jnp.maximum(minus, 0.0), -jnp.minimum(plus, 0.0))
                    down = jnp.maximum(-jnp.minimum(minus, 0.0), jnp.maximum(plus, 0.0))
                    grow_plus = up * up if grow_plus is None else grow_plus + up * up
                    grow_minus = down * down if grow_minus is None else grow_minus + down * down
                rate = speed[z, at, :]
                growth = jnp.sqrt(jnp.where(rate > 0.0, grow_plus, grow_minus))
                value = mid - TIME_STEP * (rate * growth)
                if final:
                    next_ref[z - MARGIN, pl.ds(start - SIDE, CHUNK), :] = value
                    speed_ref[z - MARGIN, pl.ds(start - SIDE, CHUNK), :] = rate
                else:
                    target[z, at, :] = settle(z, start, value, 1.0)

        pl.loop(MARGIN - margin, MARGIN + own_z + margin)(march)
        source, target = target, source


def rows_beside(block, width):
    low = shift_from(block, "narrow", 1, width, True)
    high = shift_from(block, "narrow", 1, width, False)
    return block, low, high


def march(velocity, phi, peak, own_z, own_y):
    deep, _, size_x = phi[0].shape
    place = jnp.stack(
        [
            lax.axis_index("wide") * own_z - MARGIN,
            lax.axis_size("wide") * own_z,
            lax.axis_index("narrow") * own_y - SIDE,
            lax.axis_size("narrow") * own_y,
        ]
    ).astype(jnp.int32)
    result = jax.ShapeDtypeStruct((own_z, own_y, size_x), jnp.float32)
    smem = pl.BlockSpec(memory_space=pltpu.SMEM)
    vmem = pl.BlockSpec(memory_space=pltpu.VMEM)
    return pl.pallas_call(
        march_kernel,
        out_shape=(result, result),
        in_specs=[smem, smem] + [vmem] * 6,
        out_specs=(vmem, vmem),
        scratch_shapes=[pltpu.VMEM((deep, own_y + 2 * SIDE, size_x), jnp.float32)] * 6,
        compiler_params=pltpu.CompilerParams(vmem_limit_bytes=56 << 20),
        cost_estimate=pl.CostEstimate(flops=200000000, bytes_accessed=8000000, transcendentals=0),
    )(place, jnp.reshape(peak, (1,)), *velocity, *phi)


def per_device(displacement, material, level_set):
    own_z, own_y, size_x = level_set.shape
    low = shift_from(level_set, "wide", 0, MARGIN, True)
    high = shift_from(level_set, "wide", 0, MARGIN, False)
    phi = rows_beside(jnp.concatenate([low, level_set, high], axis=0), MARGIN)
    energy, own_peak, phi = slab_energy(displacement, material, phi)
    devices = lax.axis_size("wide") * lax.axis_size("narrow")
    peaks = lax.all_to_all(
        jnp.full((devices, 1, 128), own_peak), ("wide", "narrow"), split_axis=0, concat_axis=0, tiled=True
    )
    flipped = jnp.pad(jnp.transpose(energy, (2, 1, 0)), ((MARGIN, MARGIN), (0, 0), (0, 0)))
    chunks = [
        lax.slice_in_dim(flipped, k * own_z, k * own_z + own_z + 2 * MARGIN, axis=0)
        for k in range(lax.axis_size("wide"))
    ]
    moved = lax.all_to_all(
        jnp.concatenate(chunks, axis=0), "wide", split_axis=0, concat_axis=2, tiled=True
    )
    return march(rows_beside(moved, MARGIN), phi, jnp.max(peaks), own_z, own_y)


def solution(mesh):
    return jax.shard_map(
        per_device,
        mesh=mesh,
        in_specs=(
            P(None, None, "wide", "narrow", None),
            P("wide", "narrow", None),
            P("wide", "narrow", None),
        ),
        out_specs=(P("wide", "narrow", None), P("wide", "narrow", None)),
        check_vma=False,
    )
```
